32 devices in a mesh: expert: 8 (over z, x), opt: 4 (over y, core).
Axes of the slice: x: 2, y: 2, z: 4, core: 2. Of those that a mesh axis runs over, the one named last changes fastest.
Arguments:
- out_grad: bfloat16 [16384, 2048], P(('expert', 'opt')), may hold values from -6 to 6
- saved_input: bfloat16 [16384, 768], P(('expert', 'opt')), may hold values from -6 to 6
- route: int32 [16384, 1], P(('expert', 'opt')), may hold values from 0 to 31, as said below
- place_now: int32 [32], replicated, may hold values from 0 to 7, as said below
- place_next: int32 [32], replicated, may hold values from 0 to 7, as said below
- master: float32 [8, 1572864], P(None, ('expert', 'opt')), may hold values from -0.21875 to 0.21875
- moment_one: float32 [8, 1572864], P(None, ('expert', 'opt')), may hold values from -2 to 2
- moment_two: float32 [8, 1572864], P(None, ('expert', 'opt')), may hold values from 0.01 to 1
- fwd_input: bfloat16 [32768, 768], P(('expert', 'opt')), may hold values from -6 to 6
Outputs:
- input_grad: bfloat16 [16384, 768], P(('expert', 'opt'))
- new_master: float32 [8, 1572864], P(None, ('expert', 'opt'))
- new_moment_one: float32 [8, 1572864], P(None, ('expert', 'opt'))
- new_moment_two: float32 [8, 1572864], P(None, ('expert', 'opt'))
- fwd_output: bfloat16 [32768, 2048], P(('expert', 'opt'))
The draws below stay inside these ranges and needn't reach their ends.
Inputs may be any that keep to these rules, and one draw needn't show every extreme that they name: `route`: among the 512 rows of one device, at most 32 go to one replica device; in every draw some replica device receives exactly 32 rows from every device. `place_now`: every one of the 8 experts holds at least one replica slot. `place_next`: every one of the 8 experts holds at least one replica slot.
All inputs are finite; a program needn't handle non-finite values.
Results may differ from the reference program's by a relative error of at most 0.005.
Values may be sent and summed in bfloat16 or wider, within the bound.
A program may use at most 128 MiB of HBM per device.

```python
import math
import jax
import jax.numpy as jnp
from jax import lax

D = 2048
FF = 768
TOK_DEV = 512
FWD_ROWS = 1024
EXPERTS = 8
CAP = 32
TOKENS = 16384
N_EXPERT = 8
N_OPT = 4
DEVICES = 32


def draw_route(key, part):
    device_count = N_EXPERT * N_OPT
    slot_count = device_count * CAP
    key_full, key_popular, key_blocks = jax.random.split(jax.random.fold_in(key, 11), 3)
    full_target = jax.random.randint(key_full, (), 0, device_count)
    popularity = jax.random.randint(key_popular, (device_count,), 0, 4)
    slot_owner = jnp.arange(slot_count, dtype=jnp.int32) // CAP

    def one_block(block_key):
        key_noise, key_shuffle = jax.random.split(block_key)
        noise_draw = jax.random.randint(key_noise, (slot_count,), 0, 1024)
        scores = (noise_draw + 512 * popularity[slot_owner]) * slot_count + jnp.arange(slot_count, dtype=jnp.int32)
        scores = jnp.where(slot_owner == full_target, jnp.int32(2 ** 30), scores)
        _, chosen_slots = lax.top_k(scores, TOK_DEV)
        chosen = slot_owner[chosen_slots]
        return jax.random.permutation(key_shuffle, chosen)
    blocks = jax.vmap(one_block)(jax.random.split(key_blocks, device_count))
    return blocks.reshape(TOK_DEV * device_count, 1).astype(jnp.int32)


def draw_placement(key, salt_value):
    device_count = N_EXPERT * N_OPT
    key_first, key_left, key_right, key_label, key_shuffle = jax.random.split(jax.random.fold_in(key, salt_value), 5)
    first_pass = jax.random.permutation(key_first, EXPERTS)
    relabel = jax.random.permutation(key_label, EXPERTS)
    extra_count = device_count - EXPERTS
    low_pick = jnp.minimum(jax.random.randint(key_left, (extra_count,), 0, EXPERTS), jax.random.randint(key_right, (extra_count,), 0, EXPERTS))
    extra_slots = relabel[low_pick]
    combined = jnp.concatenate([first_pass, extra_slots]).astype(jnp.int32)
    return jax.random.permutation(key_shuffle, combined).astype(jnp.int32)


def draw_place_now(key, part):
    return draw_placement(key, 3)


def draw_place_next(key, part):
    return draw_placement(key, 5)


def block_levels(key, shape, shards, least, high):
    level, own = 1.0, jax.random.fold_in(key, 6)
    for dim, parts in shards:
        draws = jnp.exp(jax.random.uniform(jax.random.fold_in(own, dim), (parts,), jnp.float32, least / len(shards), high / len(shards)))
        level = level * jnp.repeat(draws, shape[dim] // parts).reshape([-1 if axis == dim else 1 for axis in range(len(shape))])
    return level


def centred(rng, shape, spread, reach, cuts=(), kind=jnp.bfloat16):
    factor_of = block_levels(rng, shape, cuts, -0.22, 0.18) if cuts else 1.0
    entries = jax.random.normal(rng, shape, jnp.float32) * spread * factor_of
    return jnp.minimum(jnp.maximum(entries, -reach), reach).astype(kind)


def setup_inputs(seed: int = 0) -> dict:
    key_of = jax.random.split(jax.random.key(seed), 10)
    out_grad = centred(key_of[0], (TOKENS, D), 1.0, 6.0, ((0, 32),))
    saved_input = centred(key_of[1], (TOKENS, FF), 1.0, 6.0, ((0, 32),))
    route = draw_route(jax.random.fold_in(key_of[9], 71), 0)
    place_now = draw_place_now(jax.random.fold_in(key_of[9], 71), 0)
    place_next = draw_place_next(jax.random.fold_in(key_of[9], 71), 0)
    master = centred(key_of[5], (EXPERTS, FF * D), FF ** -0.5, 0.21875, ((1, 32),), jnp.float32)
    moment_one = centred(key_of[6], (EXPERTS, FF * D), 0.3, 2.0, ((1, 32),), jnp.float32)
    moment_two = jnp.clip(jnp.exp(math.log(1.0) - 4.6051702 * jax.random.uniform(key_of[7], (EXPERTS, FF * D), jnp.float32) ** block_levels(key_of[7], (EXPERTS, FF * D), ((1, 32),), -0.2, 0.2)), 0.01, 1.0)
    fwd_input = centred(key_of[8], (DEVICES * FWD_ROWS, FF), 1.0, 6.0, ((0, 32),))
    return dict(out_grad=out_grad, saved_input=saved_input, route=route, place_now=place_now, place_next=place_next, master=master, moment_one=moment_one, moment_two=moment_two, fwd_input=fwd_input)


LOSS_SCALE = 64.0
BETA_ONE = 0.9
BETA_TWO = 0.95
LEARN_RATE = 0.002
DECAY = 0.1
EPSILON = 1e-08
STEP_COUNT = 20.0

def reference(out_grad, saved_input, route, place_now, place_next, master, moment_one, moment_two, fwd_input):
    device_count = N_EXPERT * N_OPT
    window = device_count * CAP
    target = route[:, 0].astype(jnp.int32)
    sorted_order = jnp.argsort(target, stable=True).astype(jnp.int32)
    counts = lax.optimization_barrier(jnp.sum((target[:, None] == jnp.arange(device_count, dtype=jnp.int32)[None, :]).astype(jnp.int32), axis=0))
    starts = (jnp.cumsum(counts) - counts).astype(jnp.int32)
    grad_pad = jnp.concatenate([out_grad[sorted_order], jnp.zeros((window, D), out_grad.dtype)], axis=0)
    hidden_pad = jnp.concatenate([saved_input[sorted_order], jnp.zeros((window, FF), saved_input.dtype)], axis=0)
    weights_now = master.astype(jnp.bfloat16)

    def visit_replica(state_pair, replica):
        gradient_sum, input_sorted = state_pair
        start = starts[replica]
        live_mask = (jnp.arange(window, dtype=jnp.int32) < counts[replica])[:, None]
        grad_rows = lax.dynamic_slice_in_dim(grad_pad, start, window, 0)
        hidden_rows = lax.dynamic_slice_in_dim(hidden_pad, start, window, 0)
        grad_rows = jnp.where(live_mask, grad_rows, jnp.zeros_like(grad_rows))
        hidden_rows = jnp.where(live_mask, hidden_rows, jnp.zeros_like(hidden_rows))
        expert = place_now[replica]
        weight_now = lax.dynamic_index_in_dim(weights_now, expert, 0, keepdims=False).reshape(FF, D)
        partial_value = lax.dot_general(hidden_rows, grad_rows, (((0,), (0,)), ((), ())), preferred_element_type=jnp.float32)
        partial_wire = lax.optimization_barrier((partial_value / LOSS_SCALE).astype(jnp.bfloat16))
        gradient_sum = gradient_sum.at[expert].add(partial_wire.astype(jnp.float32).reshape(-1))
        input_part = lax.dot_general(grad_rows, weight_now, (((1,), (1,)), ((), ())), preferred_element_type=jnp.float32).astype(jnp.bfloat16)
        previous = lax.dynamic_slice_in_dim(input_sorted, start, window, 0)
        input_sorted = lax.dynamic_update_slice_in_dim(input_sorted, jnp.where(live_mask, input_part, previous), start, 0)
        return ((gradient_sum, input_sorted), None)
    initial = (jnp.zeros((EXPERTS, FF * D), jnp.float32), jnp.zeros((TOKENS + window, FF), jnp.bfloat16))
    (gradient, input_sorted), _ = lax.scan(visit_replica, initial, jnp.arange(device_count, dtype=jnp.int32))
    input_grad = jnp.zeros((TOKENS, FF), jnp.bfloat16).at[sorted_order].set(input_sorted[:TOKENS])
    new_moment_one = BETA_ONE * moment_one + (1.0 - BETA_ONE) * gradient
    new_moment_two = BETA_TWO * moment_two + (1.0 - BETA_TWO) * gradient * gradient
    first_hat = new_moment_one / (1.0 - BETA_ONE ** STEP_COUNT)
    second_hat = new_moment_two / (1.0 - BETA_TWO ** STEP_COUNT)
    new_master = master - LEARN_RATE * (first_hat / (jnp.sqrt(second_hat) + EPSILON) + DECAY * master)
    weights_next = new_master.astype(jnp.bfloat16)
    blocks = fwd_input.reshape(device_count, FWD_ROWS, FF)

    def forward_block(pair):
        rows_block, expert = pair
        weight_next = lax.dynamic_index_in_dim(weights_next, expert, 0, keepdims=False).reshape(FF, D)
        return jnp.dot(rows_block, weight_next, preferred_element_type=jnp.float32).astype(jnp.bfloat16)
    fwd_output = lax.map(forward_block, (blocks, place_next)).reshape(device_count * FWD_ROWS, D)
    return (input_grad, new_master, new_moment_one, new_moment_two, fwd_output)
```

```python
import jax
import jax.numpy as jnp
from jax import lax
from jax.sharding import PartitionSpec as P
from jax.experimental import pallas as pl
from jax.experimental.pallas import tpu as pltpu

LOSS_SCALE = 64.0
BETA_ONE = 0.9
BETA_TWO = 0.95
LEARN_RATE = 0.002
DECAY = 0.1
EPSILON = 1e-08
STEP_COUNT = 20.0
GATHER_BYTES = 32 * 1024 * 1024
AXES = ("expert", "opt")


def replica_weights(weights, placement, hidden_width, model_width):
    picked = jnp.take(weights.astype(jnp.bfloat16), placement, axis=0)
    arrived = lax.all_to_all(picked, ("expert", "opt"), split_axis=0, concat_axis=0, tiled=True)
    return arrived.reshape(hidden_width, model_width)


def per_device(
    out_grad, saved_input, route, place_now, place_next, master, moment_one, moment_two, fwd_input
):
    groups = lax.axis_size("expert")
    members = lax.axis_size("opt")
    device_count = groups * members
    rows_here = out_grad.shape[0]
    model_width = out_grad.shape[1]
    hidden_width = saved_input.shape[1]
    capacity = 2 * rows_here // device_count
    slot_count = device_count * capacity
    target = route[:, 0]
    matches = (target[:, None] == jnp.arange(device_count, dtype=jnp.int32)[None, :]).astype(
        jnp.int32
    )
    earlier = jnp.sum(jnp.cumsum(matches, axis=0) * matches, axis=1) - 1
    position = target * capacity + earlier
    hidden_send = jnp.zeros((slot_count, hidden_width), jnp.bfloat16).at[position].set(saved_input)
    grad_send = jnp.zeros((slot_count, model_width), jnp.bfloat16).at[position].set(out_grad)
    hidden_got, grad_got = (
        lax.all_to_all(hidden_send, ("expert", "opt"), split_axis=0, concat_axis=0, tiled=True),
        lax.all_to_all(grad_send, ("expert", "opt"), split_axis=0, concat_axis=0, tiled=True),
    )
    weight_now = replica_weights(master, place_now, hidden_width, model_width)
    input_part = lax.dot_general(
        grad_got, weight_now, (((1,), (1,)), ((), ())), preferred_element_type=jnp.float32
    ).astype(jnp.bfloat16)
    returned = lax.all_to_all(
        input_part, ("expert", "opt"), split_axis=0, concat_axis=0, tiled=True
    )
    input_grad = jnp.take(returned, position, axis=0)
    weight_part = (
        lax.dot_general(
            hidden_got, grad_got, (((0,), (0,)), ((), ())), preferred_element_type=jnp.float32
        )
        / LOSS_SCALE
    )
    pieces = weight_part.astype(jnp.bfloat16).reshape(device_count, -1)
    arrived = lax.all_to_all(pieces, ("expert", "opt"), split_axis=0, concat_axis=0, tiled=True)
    experts = master.shape[0]
    owners = (place_now[None, :] == jnp.arange(experts, dtype=jnp.int32)[:, None]).astype(
        jnp.float32
    )
    gradient = jnp.dot(
        owners,
        arrived.astype(jnp.float32),
        precision=lax.Precision.HIGHEST,
        preferred_element_type=jnp.float32,
    )
    new_moment_one = BETA_ONE * moment_one + (1.0 - BETA_ONE) * gradient
    new_moment_two = BETA_TWO * moment_two + (1.0 - BETA_TWO) * gradient * gradient
    first_hat = new_moment_one / (1.0 - BETA_ONE**STEP_COUNT)
    second_hat = new_moment_two / (1.0 - BETA_TWO**STEP_COUNT)
    new_master = master - LEARN_RATE * (
        first_hat / (jnp.sqrt(second_hat) + EPSILON) + DECAY * master
    )
    weight_next = replica_weights(new_master, place_next, hidden_width, model_width)
    fwd_output = jnp.dot(fwd_input, weight_next, preferred_element_type=jnp.float32).astype(
        jnp.bfloat16
    )
    return (input_grad, new_master, new_moment_one, new_moment_two, fwd_output)


def rows_kernel(master_ref, rows_ref):
    experts = master_ref.shape[0]
    width = rows_ref.shape[1]
    for part in range(rows_ref.shape[0] // experts):
        rows_ref[part * experts : (part + 1) * experts, :] = master_ref[
            :, part * width : (part + 1) * width
        ].astype(rows_ref.dtype)


def expert_rows(master, model_width, per_step):
    experts, flat = master.shape
    steps = flat // model_width // per_step
    return pl.pallas_call(
        rows_kernel,
        grid=(steps,),
        in_specs=[pl.BlockSpec((experts, per_step * model_width), lambda i: (0, i))],
        out_specs=pl.BlockSpec((per_step * experts, model_width), lambda i: (i, 0)),
        out_shape=jax.ShapeDtypeStruct((flat // model_width * experts, model_width), jnp.bfloat16),
    )(master)


def adamw_kernel(grad_ref, master_ref, one_ref, two_ref, master_out, one_out, two_out, rows_out):
    experts = master_ref.shape[0]
    width = grad_ref.shape[1]
    for part in range(grad_ref.shape[0] // experts):
        rows = slice(part * experts, (part + 1) * experts)
        columns = slice(part * width, (part + 1) * width)
        gradient = grad_ref[rows, :].astype(jnp.float32)
        new_one = BETA_ONE * one_ref[:, columns] + (1.0 - BETA_ONE) * gradient
        new_two = BETA_TWO * two_ref[:, columns] + (1.0 - BETA_TWO) * gradient * gradient
        first_hat = new_one / (1.0 - BETA_ONE**STEP_COUNT)
        second_hat = new_two / (1.0 - BETA_TWO**STEP_COUNT)
        master = master_ref[:, columns]
        new_master = master - LEARN_RATE * (
            first_hat / (jnp.sqrt(second_hat) + EPSILON) + DECAY * master
        )
        one_out[:, columns] = new_one
        two_out[:, columns] = new_two
        master_out[:, columns] = new_master
        rows_out[rows, :] = new_master.astype(rows_out.dtype)


def adamw(grad_rows, master, moment_one, moment_two, per_step):
    experts, flat = master.shape
    width = grad_rows.shape[1]
    steps = flat // width // per_step
    wide = pl.BlockSpec((experts, per_step * width), lambda i: (0, i))
    tall = pl.BlockSpec((per_step * experts, width), lambda i: (i, 0))
    state = jax.ShapeDtypeStruct(master.shape, jnp.float32)
    return pl.pallas_call(
        adamw_kernel,
        grid=(steps,),
        in_specs=[tall, wide, wide, wide],
        out_specs=[wide, wide, wide, tall],
        out_shape=[state, state, state, jax.ShapeDtypeStruct(grad_rows.shape, jnp.bfloat16)],
    )(grad_rows, master, moment_one, moment_two)


def gathered_device(
    out_grad, saved_input, route, place_now, place_next, master, moment_one, moment_two, fwd_input
):
    device_count = lax.axis_size("expert") * lax.axis_size("opt")
    model_width = out_grad.shape[1]
    hidden_width = saved_input.shape[1]
    rows_here = out_grad.shape[0]
    experts = master.shape[0]
    owned = hidden_width // device_count
    per_step = 4 if owned % 4 == 0 else 2
    weight_rows = lax.all_gather(
        expert_rows(master, model_width, per_step), AXES, axis=0, tiled=True
    )
    replicas = jnp.arange(device_count, dtype=jnp.int32)
    expert_of = jnp.sum(
        jnp.where(route[:, 0][None, :] == replicas[:, None], place_now[:, None], 0), axis=0
    )
    expert_ids = jnp.arange(experts, dtype=jnp.int32)
    mine = expert_of[None, :] == expert_ids[:, None]
    spread = jnp.where(
        mine[None, :, :], saved_input.T[:, None, :], jnp.zeros((), jnp.bfloat16)
    ).reshape(hidden_width * experts, rows_here)
    partial = (
        jnp.dot(spread, out_grad, preferred_element_type=jnp.float32) / LOSS_SCALE
    ).astype(jnp.bfloat16)
    grad_rows = lax.psum_scatter(partial, AXES, scatter_dimension=0, tiled=True)
    every = lax.dot_general(
        weight_rows, out_grad, (((1,), (1,)), ((), ())), preferred_element_type=jnp.float32
    ).reshape(hidden_width, experts, rows_here)
    input_grad = jnp.sum(jnp.where(mine[None, :, :], every, 0.0), axis=1).astype(jnp.bfloat16).T
    new_master, new_one, new_two, next_rows = adamw(
        grad_rows, master, moment_one, moment_two, per_step
    )
    row_ids = jnp.arange(owned, dtype=jnp.int32)
    chosen = (place_next[:, None] == expert_ids[None, :])[:, None, None, :] & (
        row_ids[:, None] == row_ids[None, :]
    )[None, :, :, None]
    picked = jnp.dot(
        chosen.reshape(device_count * owned, owned * experts).astype(jnp.bfloat16),
        next_rows,
        preferred_element_type=jnp.float32,
    ).astype(jnp.bfloat16)
    weight_next = lax.all_to_all(
        picked.reshape(device_count, owned, model_width), AXES, split_axis=0, concat_axis=0, tiled=True
    ).reshape(hidden_width, model_width)
    fwd_output = jnp.dot(fwd_input, weight_next, preferred_element_type=jnp.float32).astype(
        jnp.bfloat16
    )
    return (input_grad, new_master, new_one, new_two, fwd_output)


def one_device(*arguments):
    master = arguments[5]
    devices = lax.axis_size("expert") * lax.axis_size("opt")
    gathered = 2 * master.shape[0] * master.shape[1] * devices
    if gathered <= GATHER_BYTES:
        return gathered_device(*arguments)
    return per_device(*arguments)


def solution(mesh):
    return jax.shard_map(
        one_device,
        mesh=mesh,
        in_specs=(
            P(("expert", "opt"), None),
            P(("expert", "opt"), None),
            P(("expert", "opt"), None),
            P(),
            P(),
            P(None, ("expert", "opt")),
            P(None, ("expert", "opt")),
            P(None, ("expert", "opt")),
            P(("expert", "opt"), None),
        ),
        out_specs=(
            P(("expert", "opt"), None),
            P(None, ("expert", "opt")),
            P(None, ("expert", "opt")),
            P(None, ("expert", "opt")),
            P(("expert", "opt"), None),
        ),
        check_vma=False,
    )
```

```python
import jax
import jax.numpy as jnp
from jax import lax
from jax.sharding import PartitionSpec as P
from jax.experimental import pallas as pl

LOSS_SCALE = 64.0
BETA_ONE = 0.9
BETA_TWO = 0.95
LEARN_RATE = 0.002
DECAY = 0.1
EPSILON = 1e-08
STEP_COUNT = 20.0
AXES = ("expert", "opt")


def rows_kernel(master_ref, rows_ref):
    experts = master_ref.shape[0]
    width = rows_ref.shape[1]
    for part in range(rows_ref.shape[0] // experts):
        rows_ref[part * experts : (part + 1) * experts, :] = master_ref[
            :, part * width : (part + 1) * width
        ].astype(rows_ref.dtype)


def expert_rows(master, model_width, per_step):
    experts, flat = master.shape
    steps = flat // model_width // per_step
    return pl.pallas_call(
        rows_kernel,
        grid=(steps,),
        in_specs=[pl.BlockSpec((experts, per_step * model_width), lambda i: (0, i))],
        out_specs=pl.BlockSpec((per_step * experts, model_width), lambda i: (i, 0)),
        out_shape=jax.ShapeDtypeStruct((flat // model_width * experts, model_width), jnp.bfloat16),
    )(master)


def adamw_kernel(grad_ref, master_ref, one_ref, two_ref, master_out, one_out, two_out, rows_out):
    experts = master_ref.shape[0]
    width = grad_ref.shape[1]
    for part in range(grad_ref.shape[0] // experts):
        rows = slice(part * experts, (part + 1) * experts)
        columns = slice(part * width, (part + 1) * width)
        gradient = grad_ref[rows, :].astype(jnp.float32)
        new_one = BETA_ONE * one_ref[:, columns] + (1.0 - BETA_ONE) * gradient
        new_two = BETA_TWO * two_ref[:, columns] + (1.0 - BETA_TWO) * gradient * gradient
        first_hat = new_one / (1.0 - BETA_ONE**STEP_COUNT)
        second_hat = new_two / (1.0 - BETA_TWO**STEP_COUNT)
        master = master_ref[:, columns]
        new_master = master - LEARN_RATE * (
            first_hat / (jnp.sqrt(second_hat) + EPSILON) + DECAY * master
        )
        one_out[:, columns] = new_one
        two_out[:, columns] = new_two
        master_out[:, columns] = new_master
        rows_out[rows, :] = new_master.astype(rows_out.dtype)


def adamw(grad_rows, master, moment_one, moment_two, per_step):
    experts, flat = master.shape
    width = grad_rows.shape[1]
    steps = flat // width // per_step
    wide = pl.BlockSpec((experts, per_step * width), lambda i: (0, i))
    tall = pl.BlockSpec((per_step * experts, width), lambda i: (i, 0))
    state = jax.ShapeDtypeStruct(master.shape, jnp.float32)
    return pl.pallas_call(
        adamw_kernel,
        grid=(steps,),
        in_specs=[tall, wide, wide, wide],
        out_specs=[wide, wide, wide, tall],
        out_shape=[state, state, state, jax.ShapeDtypeStruct(grad_rows.shape, jnp.bfloat16)],
    )(grad_rows, master, moment_one, moment_two)


def exchange(blocks):
    return lax.all_to_all(blocks, AXES, split_axis=0, concat_axis=0, tiled=True)


def owner_choice(placement, experts, owned):
    expert_ids = jnp.arange(experts, dtype=jnp.int32)
    row_ids = jnp.arange(owned, dtype=jnp.int32)
    chosen = (placement[:, None] == expert_ids[None, :])[:, None, None, :] & (
        row_ids[:, None] == row_ids[None, :]
    )[None, :, :, None]
    return chosen.reshape(placement.shape[0] * owned, owned * experts).astype(jnp.bfloat16)


def select(choice, rows):
    return jnp.dot(choice, rows, preferred_element_type=jnp.float32).astype(jnp.bfloat16)


def replica_weights(choice, rows, device_count):
    picked = select(choice, rows)
    width = picked.shape[1]
    return exchange(picked.reshape(device_count, -1, width)).reshape(-1, width)


def matmul_kernel(left_ref, right_ref, out_ref):
    out_ref[...] = jnp.dot(
        left_ref[...], right_ref[...], preferred_element_type=jnp.float32
    ).astype(out_ref.dtype)


def matmul(left, right, steps):
    rows, depth = left.shape
    width = right.shape[1]
    return pl.pallas_call(
        matmul_kernel,
        grid=(steps,),
        in_specs=[
            pl.BlockSpec((rows // steps, depth), lambda i: (i, 0)),
            pl.BlockSpec((depth, width), lambda i: (0, 0)),
        ],
        out_specs=pl.BlockSpec((rows // steps, width), lambda i: (i, 0)),
        out_shape=jax.ShapeDtypeStruct((rows, width), left.dtype),
    )(left, right)


def per_device(
    out_grad, saved_input, route, place_now, place_next, master, moment_one, moment_two, fwd_input
):
    device_count = lax.axis_size("expert") * lax.axis_size("opt")
    rows_here, model_width = out_grad.shape
    hidden_width = saved_input.shape[1]
    experts = master.shape[0]
    owned = hidden_width // device_count
    per_step = 4 if owned % 4 == 0 else 2
    capacity = 2 * rows_here // device_count
    slot_count = device_count * capacity
    target = route[:, 0]
    matches = (target[:, None] == jnp.arange(device_count, dtype=jnp.int32)[None, :]).astype(
        jnp.int32
    )
    earlier = jnp.sum(jnp.cumsum(matches, axis=0) * matches, axis=1) - 1
    position = target * capacity + earlier
    slots = (
        jnp.arange(slot_count, dtype=jnp.int32)[:, None] == position[None, :]
    ).astype(jnp.bfloat16)
    hidden_got = exchange(
        select(slots, saved_input).reshape(device_count, capacity, hidden_width)
    ).reshape(slot_count, hidden_width)
    grad_got = exchange(
        select(slots, out_grad).reshape(device_count, capacity, model_width)
    ).reshape(slot_count, model_width)
    partial = (
        lax.dot_general(
            hidden_got, grad_got, (((0,), (0,)), ((), ())), preferred_element_type=jnp.float32
        )
        / LOSS_SCALE
    ).astype(jnp.bfloat16)
    arrived = exchange(partial.reshape(device_count, owned, model_width)).reshape(
        hidden_width, model_width
    )
    choice_now = owner_choice(place_now, experts, owned)
    grad_rows = lax.dot_general(
        choice_now, arrived, (((0,), (0,)), ((), ())), preferred_element_type=jnp.float32
    )
    weight_now = replica_weights(
        choice_now, expert_rows(master, model_width, per_step), device_count
    )
    input_part = lax.dot_general(
        grad_got, weight_now, (((1,), (1,)), ((), ())), preferred_element_type=jnp.float32
    ).astype(jnp.bfloat16)
    returned = exchange(input_part.reshape(device_count, capacity, hidden_width)).reshape(
        slot_count, hidden_width
    )
    input_grad = lax.dot_general(
        slots, returned, (((0,), (0,)), ((), ())), preferred_element_type=jnp.float32
    ).astype(jnp.bfloat16)
    new_master, new_one, new_two, next_rows = adamw(
        grad_rows, master, moment_one, moment_two, per_step
    )
    weight_next = replica_weights(
        owner_choice(place_next, experts, owned), next_rows, device_count
    )
    fwd_output = matmul(fwd_input, weight_next, 4)
    return (input_grad, new_master, new_one, new_two, fwd_output)


def solution(mesh):
    return jax.shard_map(
        per_device,
        mesh=mesh,
        in_specs=(
            P(("expert", "opt"), None),
            P(("expert", "opt"), None),
            P(("expert", "opt"), None),
            P(),
            P(),
            P(None, ("expert", "opt")),
            P(None, ("expert", "opt")),
            P(None, ("expert", "opt")),
            P(("expert", "opt"), None),
        ),
        out_specs=(
            P(("expert", "opt"), None),
            P(None, ("expert", "opt")),
            P(None, ("expert", "opt")),
            P(None, ("expert", "opt")),
            P(("expert", "opt"), None),
        ),
        check_vma=False,
    )
```

```python
import functools

import jax
import jax.numpy as jnp
from jax import lax
from jax.sharding import PartitionSpec as P
from jax.experimental import pallas as pl
from jax.experimental.pallas import tpu as pltpu

LOSS_SCALE = 64.0
BETA_ONE = 0.9
BETA_TWO = 0.95
LEARN_RATE = 0.002
DECAY = 0.1
EPSILON = 1e-08
STEP_COUNT = 20.0
AXES = ("expert", "opt")


def rows_kernel(master_ref, rows_ref):
    experts = master_ref.shape[0]
    width = rows_ref.shape[1]
    for part in range(rows_ref.shape[0] // experts):
        rows_ref[part * experts : (part + 1) * experts, :] = master_ref[
            :, part * width : (part + 1) * width
        ].astype(rows_ref.dtype)


def expert_rows(master, model_width, per_step):
    experts, flat = master.shape
    steps = flat // model_width // per_step
    return pl.pallas_call(
        rows_kernel,
        grid=(steps,),
        in_specs=[pl.BlockSpec((experts, per_step * model_width), lambda i: (0, i))],
        out_specs=pl.BlockSpec((per_step * experts, model_width), lambda i: (i, 0)),
        out_shape=jax.ShapeDtypeStruct((flat // model_width * experts, model_width), jnp.bfloat16),
    )(master)


def adamw_kernel(grad_ref, master_ref, one_ref, two_ref, master_out, one_out, two_out, rows_out):
    experts = master_ref.shape[0]
    width = grad_ref.shape[1]
    for part in range(grad_ref.shape[0] // experts):
        rows = slice(part * experts, (part + 1) * experts)
        columns = slice(part * width, (part + 1) * width)
        gradient = grad_ref[rows, :].astype(jnp.float32)
        new_one = BETA_ONE * one_ref[:, columns] + (1.0 - BETA_ONE) * gradient
        new_two = BETA_TWO * two_ref[:, columns] + (1.0 - BETA_TWO) * gradient * gradient
        first_hat = new_one / (1.0 - BETA_ONE**STEP_COUNT)
        second_hat = new_two / (1.0 - BETA_TWO**STEP_COUNT)
        master = master_ref[:, columns]
        new_master = master - LEARN_RATE * (
            first_hat / (jnp.sqrt(second_hat) + EPSILON) + DECAY * master
        )
        one_out[:, columns] = new_one
        two_out[:, columns] = new_two
        master_out[:, columns] = new_master
        rows_out[rows, :] = new_master.astype(rows_out.dtype)


def adamw(grad_rows, master, moment_one, moment_two, per_step):
    experts, flat = master.shape
    width = grad_rows.shape[1]
    steps = flat // width // per_step
    wide = pl.BlockSpec((experts, per_step * width), lambda i: (0, i))
    tall = pl.BlockSpec((per_step * experts, width), lambda i: (i, 0))
    state = jax.ShapeDtypeStruct(master.shape, jnp.float32)
    return pl.pallas_call(
        adamw_kernel,
        grid=(steps,),
        in_specs=[tall, wide, wide, wide],
        out_specs=[wide, wide, wide, tall],
        out_shape=[state, state, state, jax.ShapeDtypeStruct(grad_rows.shape, jnp.bfloat16)],
    )(grad_rows, master, moment_one, moment_two)


def exchange(blocks):
    return lax.all_to_all(blocks, AXES, split_axis=0, concat_axis=0, tiled=True)


def exchange_kernel(count, members, *refs):
    device_count = refs[0].shape[0]
    sources, targets = refs[:count], refs[count : 2 * count]
    send_sem, recv_sem, own_sem = refs[2 * count :]
    me = lax.axis_index("expert") * members + lax.axis_index("opt")
    barrier = pltpu.get_barrier_semaphore()

    def coordinates(step):
        other = lax.rem(me + step, device_count)
        return other, (other // members, lax.rem(other, members))

    def greet(step, carry):
        pl.semaphore_signal(
            barrier,
            inc=1,
            device_id=coordinates(step)[1],
            device_id_type=pl.DeviceIdType.MESH,
        )
        return carry

    lax.fori_loop(1, device_count, greet, 0)
    pl.semaphore_wait(barrier, device_count - 1)
    own = [
        pltpu.make_async_copy(sources[k].at[me], targets[k].at[me], own_sem.at[k])
        for k in range(count)
    ]

    def copy(k, step):
        other, place = coordinates(step)
        return pltpu.make_async_remote_copy(
            src_ref=sources[k].at[other],
            dst_ref=targets[k].at[me],
            send_sem=send_sem.at[k, step],
            recv_sem=recv_sem.at[k, step],
            device_id=place,
            device_id_type=pl.DeviceIdType.MESH,
        )

    def start(step, carry):
        for k in range(count):
            copy(k, step).start()
        return carry

    def finish(step, carry):
        for k in range(count):
            copy(k, step).wait()
        return carry

    lax.fori_loop(1, device_count, start, 0)
    for piece in own:
        piece.start()
    for piece in own:
        piece.wait()
    lax.fori_loop(1, device_count, finish, 0)


def exchange_together(*blocks):
    count, device_count = len(blocks), blocks[0].shape[0]
    return pl.pallas_call(
        functools.partial(exchange_kernel, count, lax.axis_size("opt")),
        in_specs=[pl.BlockSpec(memory_space=pl.ANY)] * count,
        out_specs=[pl.BlockSpec(memory_space=pl.ANY)] * count,
        out_shape=[jax.ShapeDtypeStruct(block.shape, block.dtype) for block in blocks],
        scratch_shapes=[
            pltpu.SemaphoreType.DMA((count, device_count)),
            pltpu.SemaphoreType.DMA((count, device_count)),
            pltpu.SemaphoreType.DMA((count,)),
        ],
        compiler_params=pltpu.CompilerParams(collective_id=0, has_side_effects=True),
    )(*blocks)


def owner_choice(placement, experts, owned):
    expert_ids = jnp.arange(experts, dtype=jnp.int32)
    row_ids = jnp.arange(owned, dtype=jnp.int32)
    chosen = (placement[:, None] == expert_ids[None, :])[:, None, None, :] & (
        row_ids[:, None] == row_ids[None, :]
    )[None, :, :, None]
    return chosen.reshape(placement.shape[0] * owned, owned * experts).astype(jnp.bfloat16)


def select(choice, rows):
    return jnp.dot(choice, rows, preferred_element_type=jnp.float32).astype(jnp.bfloat16)


def replica_weights(choice, rows, device_count):
    picked = select(choice, rows)
    width = picked.shape[1]
    return exchange(picked.reshape(device_count, -1, width)).reshape(-1, width)


def matmul_kernel(left_ref, right_ref, out_ref):
    out_ref[...] = jnp.dot(
        left_ref[...], right_ref[...], preferred_element_type=jnp.float32
    ).astype(out_ref.dtype)


def matmul(left, right, steps):
    rows, depth = left.shape
    width = right.shape[1]
    return pl.pallas_call(
        matmul_kernel,
        grid=(steps,),
        in_specs=[
            pl.BlockSpec((rows // steps, depth), lambda i: (i, 0)),
            pl.BlockSpec((depth, width), lambda i: (0, 0)),
        ],
        out_specs=pl.BlockSpec((rows // steps, width), lambda i: (i, 0)),
        out_shape=jax.ShapeDtypeStruct((rows, width), left.dtype),
    )(left, right)


def per_device(
    out_grad, saved_input, route, place_now, place_next, master, moment_one, moment_two, fwd_input
):
    device_count = lax.axis_size("expert") * lax.axis_size("opt")
    rows_here, model_width = out_grad.shape
    hidden_width = saved_input.shape[1]
    experts = master.shape[0]
    owned = hidden_width // device_count
    per_step = 4 if owned % 4 == 0 else 2
    capacity = 2 * rows_here // device_count
    slot_count = device_count * capacity
    target = route[:, 0]
    matches = (target[:, None] == jnp.arange(device_count, dtype=jnp.int32)[None, :]).astype(
        jnp.int32
    )
    earlier = jnp.sum(jnp.cumsum(matches, axis=0) * matches, axis=1) - 1
    position = target * capacity + earlier
    slots = (
        jnp.arange(slot_count, dtype=jnp.int32)[:, None] == position[None, :]
    ).astype(jnp.bfloat16)
    choice_now = owner_choice(place_now, experts, owned)
    picked_now = select(choice_now, expert_rows(master, model_width, per_step))
    hidden_got, grad_got, weight_now = exchange_together(
        select(slots, saved_input).reshape(device_count, capacity, hidden_width),
        select(slots, out_grad).reshape(device_count, capacity, model_width),
        picked_now.reshape(device_count, owned, model_width),
    )
    hidden_got = hidden_got.reshape(slot_count, hidden_width)
    grad_got = grad_got.reshape(slot_count, model_width)
    weight_now = weight_now.reshape(hidden_width, model_width)
    partial = (
        lax.dot_general(
            hidden_got, grad_got, (((0,), (0,)), ((), ())), preferred_element_type=jnp.float32
        )
        / LOSS_SCALE
    ).astype(jnp.bfloat16)
    arrived = exchange(partial.reshape(device_count, owned, model_width)).reshape(
        hidden_width, model_width
    )
    grad_rows = lax.dot_general(
        choice_now, arrived, (((0,), (0,)), ((), ())), preferred_element_type=jnp.float32
    )
    input_part = lax.dot_general(
        grad_got, weight_now, (((1,), (1,)), ((), ())), preferred_element_type=jnp.float32
    ).astype(jnp.bfloat16)
    returned = exchange(input_part.reshape(device_count, capacity, hidden_width)).reshape(
        slot_count, hidden_width
    )
    input_grad = lax.dot_general(
        slots, returned, (((0,), (0,)), ((), ())), preferred_element_type=jnp.float32
    ).astype(jnp.bfloat16)
    new_master, new_one, new_two, next_rows = adamw(
        grad_rows, master, moment_one, moment_two, per_step
    )
    weight_next = replica_weights(
        owner_choice(place_next, experts, owned), next_rows, device_count
    )
    fwd_output = matmul(fwd_input, weight_next, 4)
    return (input_grad, new_master, new_one, new_two, fwd_output)


def solution(mesh):
    return jax.shard_map(
        per_device,
        mesh=mesh,
        in_specs=(
            P(("expert", "opt"), None),
            P(("expert", "opt"), None),
            P(("expert", "opt"), None),
            P(),
            P(),
            P(None, ("expert", "opt")),
            P(None, ("expert", "opt")),
            P(None, ("expert", "opt")),
            P(("expert", "opt"), None),
        ),
        out_specs=(
            P(("expert", "opt"), None),
            P(None, ("expert", "opt")),
            P(None, ("expert", "opt")),
            P(None, ("expert", "opt")),
            P(("expert", "opt"), None),
        ),
        check_vma=False,
    )
```
